32 devices in a mesh: chan: 4 (over y, x), space: 4 (over z), rep: 2 (over core).
Axes of the slice: x: 2, y: 2, z: 4, core: 2. Of those that a mesh axis runs over, the one named last changes fastest.
Arguments:
- inputs: bfloat16 [2, 2, 16, 512, 128], P('rep', None, 'space', 'chan'), may hold values from -6 to 6
- grad_out: bfloat16 [2, 2, 16, 512, 128], P('rep', None, 'space', 'chan'), may hold values from -6 to 6
- weight: bfloat16 [3, 3, 3, 512, 512], P(None, None, None, 'chan'), may hold values from -0.0546875 to 0.0546875
Outputs:
- grad_in: bfloat16 [2, 2, 16, 512, 128], P('rep', None, 'space', 'chan')
- grad_weight: float32 [3, 3, 3, 512, 512], P(None, None, None, ('chan', 'rep'))
The draws below stay inside these ranges and needn't reach their ends.
All inputs are finite; a program needn't handle non-finite values.
Results may differ from the reference program's by a relative error of at most 0.0031.
Values may be sent and summed in bfloat16 or wider, within the bound.
A program may use at most 64 MiB of HBM per device.

```python
import jax
import jax.numpy as jnp

CIN = 512
COUT = 512
FRAMES = 2
WIDTH = 128
HEIGHT = 16
CLIPS = 2


def level_of(rng, extent, split, least, high):
    level = 1.0
    for dim, shards_of in split:
        heights = jax.random.uniform(jax.random.fold_in(jax.random.fold_in(rng, 6), dim), (shards_of,), jnp.float32, least / len(split), high / len(split))
        level = level * jnp.repeat(jnp.exp(heights), extent[dim] // shards_of).reshape((-1,) + (1,) * (len(extent) - 1 - dim))
    return level


def gaussian(stream_key, dims, width, most, split=(), kind=jnp.bfloat16):
    factor_of = level_of(stream_key, dims, split, -0.22, 0.18) if split else 1.0
    values = jax.random.normal(stream_key, dims, jnp.float32) * width * factor_of
    return jnp.minimum(jnp.maximum(values, -most), most).astype(kind)


def setup_inputs(seed: int = 0) -> dict:
    keys = jax.random.split(jax.random.key(seed), 4)
    return {
        "inputs": gaussian(keys[0], (CLIPS, FRAMES, HEIGHT, CIN, WIDTH), 1.0, 6.0, ((0, 2), (2, 4), (3, 4))),
        "grad_out": gaussian(keys[1], (CLIPS, FRAMES, HEIGHT, COUT, WIDTH), 1.0, 6.0, ((0, 2), (2, 4), (3, 4))),
        "weight": gaussian(keys[2], (3, 3, 3, COUT, CIN), (27 * CIN) ** -0.5, 0.0546875, ((3, 4),)),
    }


def reference(inputs, grad_out, weight):
    activated = jax.nn.silu(inputs.astype(jnp.float32)).astype(jnp.bfloat16)
    active_pad = jnp.pad(activated, ((0, 0), (2, 0), (1, 1), (0, 0), (1, 1))).astype(jnp.float32)
    grad_pad = jnp.pad(grad_out, ((0, 0), (0, 2), (1, 1), (0, 0), (1, 1))).astype(jnp.float32)
    grad_full = grad_out.astype(jnp.float32)
    weight_full = weight.astype(jnp.float32)
    clip_count, frame_count, row_count, in_width, col_count = inputs.shape
    active_grad = jnp.zeros(inputs.shape, jnp.float32)
    tap_terms = []
    for frame_tap in range(3):
        for row_tap in range(3):
            for col_tap in range(3):
                window = active_pad[:, frame_tap:frame_tap + frame_count, row_tap:row_tap + row_count, :, col_tap:col_tap + col_count]
                tap_terms.append(jnp.einsum("cthiw,cthow->oi", window, grad_full))
                shifted = grad_pad[:, 2 - frame_tap:2 - frame_tap + frame_count, 2 - row_tap:2 - row_tap + row_count, :, 2 - col_tap:2 - col_tap + col_count]
                active_grad = active_grad + jnp.einsum("cthow,oi->cthiw", shifted, weight_full[frame_tap, row_tap, col_tap])
    grad_weight = jnp.stack(tap_terms).reshape(3, 3, 3, grad_out.shape[3], in_width) * (1.0 / 256.0)
    values = inputs.astype(jnp.float32)
    logistic = jax.nn.sigmoid(values)
    slope = logistic * (1.0 + values * (1.0 - logistic))
    grad_in = (active_grad * slope).astype(jnp.bfloat16)
    return grad_in, grad_weight
```

```python
import functools

import jax
import jax.numpy as jnp
from jax import lax
from jax.experimental import pallas as pl
from jax.experimental.pallas import tpu as pltpu
from jax.sharding import PartitionSpec as P

MESH = pl.DeviceIdType.MESH
F32 = jnp.float32
BF16 = jnp.bfloat16
LANES = 128


def flip(index, mask, count):
    out, bit = 0, 1
    while bit < count:
        out = out + (((index // bit) + ((mask // bit) % 2)) % 2) * bit
        bit *= 2
    return out


def nt(a, b):
    return lax.dot_general(a, b, (((1,), (1,)), ((), ())), preferred_element_type=F32)


def tn(a, b):
    return lax.dot_general(a, b, (((0,), (0,)), ((), ())), preferred_element_type=F32)


def kernel(
    cfg,
    x_ref, g_ref, w_hbm,
    gi_ref, gw_ref,
    act, halo_top, halo_bot, sib_top, sib_bot, sib_rows,
    xd, xw, w_ref, part, right_buf, left_buf, total,
    d_acc, d_send, d_recv,
    w_sem, g_send, g_recv, a_send, a_recv, b_send, b_recv,
    r_send, r_recv, l_send, l_recv, fr_send, fl_send, f_recv, d_ssem, d_rsem,
):
    n_c, n_s, frames, rows, in_part, out_part, cols, in_all = cfg
    half = out_part // 2
    first = max(0, 3 - frames)
    taps = 3 - first
    plane = rows * cols
    cells = frames * plane
    width = max(LANES, in_part)
    blocks = in_all // width
    per = width // in_part
    grad_rows = taps * 9 * half
    own_count = max(n for n in range(1, n_s + 1) if grad_rows % (16 * n) == 0)
    piece = grad_rows // own_count

    chan = lax.axis_index("chan")
    space = lax.axis_index("space")
    rep = lax.axis_index("rep")
    other = 1 - rep
    has_left = space > 0
    has_right = space < n_s - 1
    after = (space + 1) % n_s
    before = (space + n_s - 1) % n_s

    def remote(src, dst, ssem, rsem, **where):
        return pltpu.make_async_remote_copy(
            src_ref=src, dst_ref=dst, send_sem=ssem, recv_sem=rsem,
            device_id=where, device_id_type=MESH,
        )

    weight_copy = pltpu.make_async_copy(
        w_hbm.at[pl.ds(first * 9 * out_part, taps * 9 * out_part)], w_ref, w_sem
    )
    weight_copy.start()

    barrier = pltpu.get_barrier_semaphore()

    def greet(**where):
        pl.semaphore_signal(barrier, inc=1, device_id=where, device_id_type=MESH)

    for k in range(1, n_c):
        greet(chan=flip(chan, k, n_c))
    greet(rep=other)

    @pl.when(has_left)
    def _():
        greet(space=before)
        greet(space=before, rep=other)

    @pl.when(has_right)
    def _():
        greet(space=after)
        greet(space=after, rep=other)

    my_rows = pl.ds(pl.multiple_of(chan * in_part, in_part), in_part)
    for t in range(frames):
        for h in range(rows):
            v = x_ref[t, h].astype(F32)
            at = (t * rows + h) * cols
            act[0, my_rows, at : at + cols] = (v * jax.nn.sigmoid(v)).astype(BF16)

    inner = jnp.logical_and(has_left, has_right)

    @pl.when(inner)
    def _():
        pl.semaphore_wait(barrier, n_c + 4)

    @pl.when(jnp.logical_not(inner))
    def _():
        pl.semaphore_wait(barrier, n_c + (2 if n_s > 1 else 0))

    theirs = pl.ds(pl.multiple_of(other * half, half), half)

    def down():
        return remote(g_ref.at[:, rows - 1], halo_top, g_send.at[0], g_recv.at[0], space=after)

    def down_sib():
        return remote(g_ref.at[:, rows - 1, theirs], sib_top, g_send.at[1], g_recv.at[1], space=after, rep=other)

    def up():
        return remote(g_ref.at[:, 0], halo_bot, g_send.at[2], g_recv.at[2], space=before)

    def up_sib():
        return remote(g_ref.at[:, 0, theirs], sib_bot, g_send.at[3], g_recv.at[3], space=before, rep=other)

    def across():
        return remote(g_ref.at[:, :, theirs], sib_rows, g_send.at[4], g_recv.at[4], rep=other)

    @pl.when(has_right)
    def _():
        down().start()
        down_sib().start()

    @pl.when(has_left)
    def _():
        up().start()
        up_sib().start()

    across().start()

    def chan_rows(k):
        owner = flip(chan, k, n_c)
        return pl.ds(pl.multiple_of(owner * in_part, in_part), in_part)

    def relay(k):
        return remote(act.at[0, chan_rows(k)], act.at[1, chan_rows(k)], b_send.at[k], b_recv.at[k], rep=other)

    def spread(k):
        return remote(act.at[0, my_rows], act.at[0, my_rows], a_send.at[k], a_recv.at[k], chan=flip(chan, k, n_c))

    relay(0).start()
    for k in range(1, n_c):
        spread(k).start()

    @pl.when(has_left)
    def _():
        down().wait_recv()
        down_sib().wait_recv()

    @pl.when(jnp.logical_not(has_left))
    def _():
        halo_top[...] = jnp.zeros_like(halo_top)
        sib_top[...] = jnp.zeros_like(sib_top)

    @pl.when(has_right)
    def _():
        up().wait_recv()
        up_sib().wait_recv()

    @pl.when(jnp.logical_not(has_right))
    def _():
        halo_bot[...] = jnp.zeros_like(halo_bot)
        sib_bot[...] = jnp.zeros_like(sib_bot)

    across().wait_recv()

    def shifts(row):
        v = row.astype(F32)
        lane = lax.broadcasted_iota(jnp.int32, v.shape, 1)
        ahead = jnp.where(lane < cols - 1, pltpu.roll(v, cols - 1, 1), 0.0)
        behind = jnp.where(lane > 0, pltpu.roll(v, 1, 1), 0.0)
        return ahead.astype(BF16), row, behind.astype(BF16)

    def lay(dst, top, bottom, middle):
        for t in range(frames):
            for p in range(rows + 2):
                row = top(t) if p == 0 else bottom(t) if p == rows + 1 else middle(t, p - 1)
                moved = shifts(row)
                for b in range(3):
                    h = p + b - 2
                    if 0 <= h < rows:
                        at = (t * rows + h) * cols
                        for e in range(3):
                            dst(b * 3 + e, at, moved[e])

    def to_sib(i, at, value):
        xw[1, i * half : (i + 1) * half, at : at + cols] = value

    def to_own(i, at, value):
        xd[i * out_part : (i + 1) * out_part, at : at + cols] = value

    lay(to_sib, lambda t: sib_top[t], lambda t: sib_bot[t], lambda t, h: sib_rows[t, h])
    lay(to_own, lambda t: halo_top[t], lambda t: halo_bot[t], lambda t, h: g_ref[t, h])
    for i in range(9):
        xw[0, i * half : (i + 1) * half, :] = xd[
            pl.ds(pl.multiple_of(i * out_part + rep * half, half), half), :
        ]

    def block_of(j):
        return flip(chan // per, j, blocks)

    def kernel_grad(j):
        where = pl.ds(pl.multiple_of(block_of(j) * width, width), width)
        for a in range(first, 3):
            skip, used = (2 - a) * plane, (frames - 2 + a) * plane
            value = nt(xw[0, :, skip:cells], act[0, where, 0:used])
            value = value + nt(xw[1, :, skip:cells], act[1, where, 0:used])
            at = (a - first) * 9 * half
            part[j, at : at + 9 * half, :] = value

    def fetch(j):
        for k in range(j * per, (j + 1) * per):
            if k:
                spread(k).wait_recv()
                relay(k).start()

    def settle(j):
        for k in range(j * per, (j + 1) * per):
            relay(k).wait_recv()

    def rows_of(q):
        return pl.ds(pl.multiple_of(q * piece, piece), piece)

    def go_right(j, q):
        return remote(right_buf.at[j, q], right_buf.at[j, q], r_send.at[j, q], r_recv.at[j, q], space=after)

    def go_left(j, q):
        return remote(left_buf.at[j, q], left_buf.at[j, q], l_send.at[j, q], l_recv.at[j, q], space=before)

    def slot(j, q):
        return total.at[rows_of(q), pl.ds(pl.multiple_of(block_of(j) * width, width), width)]

    def final_right(j, q):
        return remote(slot(j, q), slot(j, q), fr_send.at[j, q], f_recv.at[j, q], space=after)

    def final_left(j, q):
        return remote(slot(j, q), slot(j, q), fl_send.at[j, q], f_recv.at[j, q], space=before)

    def step_right(j, q):
        @pl.when(jnp.logical_and(space < q, has_left))
        def _():
            go_right(j, q).wait_recv()
            right_buf[j, q] = (right_buf[j, q].astype(F32) + part[j, rows_of(q), :]).astype(BF16)

        @pl.when(jnp.logical_and(space < q, jnp.logical_not(has_left)))
        def _():
            right_buf[j, q] = part[j, rows_of(q), :].astype(BF16)

        @pl.when(space < q)
        def _():
            go_right(j, q).start()

    def step_left(j, q):
        @pl.when(jnp.logical_and(space > q, has_right))
        def _():
            go_left(j, q).wait_recv()
            left_buf[j, q] = (left_buf[j, q].astype(F32) + part[j, rows_of(q), :]).astype(BF16)

        @pl.when(jnp.logical_and(space > q, jnp.logical_not(has_right)))
        def _():
            left_buf[j, q] = part[j, rows_of(q), :].astype(BF16)

        @pl.when(space > q)
        def _():
            go_left(j, q).start()

    def each(count, body):
        def run(i, carry):
            body(i)
            return carry

        lax.fori_loop(0, count, run, 0)

    def reduce_pass(j):
        def body(m):
            step_right(j, own_count - 1 - m)
            step_left(j, m)

        each(own_count, body)

    def finish(j):
        @pl.when(space < own_count)
        def _():
            q = space

            @pl.when(has_left)
            def _():
                go_right(j, q).wait_recv()
                part[j, rows_of(q), :] = part[j, rows_of(q), :] + right_buf[j, q].astype(F32)

            @pl.when(has_right)
            def _():
                go_left(j, q).wait_recv()
                part[j, rows_of(q), :] = part[j, rows_of(q), :] + left_buf[j, q].astype(F32)

            slot(j, q)[...] = part[j, rows_of(q), :].astype(BF16)

            @pl.when(has_right)
            def _():
                final_right(j, q).start()

            @pl.when(has_left)
            def _():
                final_left(j, q).start()

    def share(j):
        def body(m):
            low = space - 1 - m

            @pl.when(jnp.logical_and(low >= 0, low < own_count))
            def _():
                final_right(j, low).wait_recv()

                @pl.when(has_right)
                def _():
                    final_right(j, low).start()

            high = space + 1 + m

            @pl.when(high < own_count)
            def _():
                final_left(j, high).wait_recv()

                @pl.when(has_left)
                def _():
                    final_left(j, high).start()

        each(n_s - 1, body)

    def drain(j):
        def body(q):
            @pl.when(space < q)
            def _():
                go_right(j, q).wait_send()

            @pl.when(space > q)
            def _():
                go_left(j, q).wait_send()

            @pl.when(jnp.logical_and(space >= q, has_right))
            def _():
                final_right(j, q).wait_send()

            @pl.when(jnp.logical_and(space <= q, has_left))
            def _():
                final_left(j, q).wait_send()

        each(own_count, body)

    def give(k):
        return remote(d_send.at[chan_rows(k)], d_recv.at[k], d_ssem.at[k], d_rsem.at[k], chan=flip(chan, k, n_c))

    def input_grad():
        weight_copy.wait()
        for i in range(0, in_all, width):
            for a in reversed(range(first, 3)):
                at = (a - first) * 9 * out_part
                skip, used = (2 - a) * plane, (frames - 2 + a) * plane
                value = tn(w_ref[at : at + 9 * out_part, i : i + width], xd[:, skip:cells])
                if a < 2:
                    value = value + d_acc[i : i + width, 0:used]
                d_acc[i : i + width, 0:used] = value
            d_send[i : i + width, :] = d_acc[i : i + width, :].astype(BF16)
        for k in range(1, n_c):
            give(k).start()

    def input_grad_end():
        for k in range(1, n_c):
            give(k).wait_recv()
        for t in range(frames):
            for h in range(rows):
                at = (t * rows + h) * cols
                value = d_acc[my_rows, at : at + cols]
                for k in range(1, n_c):
                    value = value + d_recv[k, :, at : at + cols].astype(F32)
                v = x_ref[t, h].astype(F32)
                s = jax.nn.sigmoid(v)
                gi_ref[t, h] = (value * (s * (1.0 + v * (1.0 - s)))).astype(BF16)

    for j in range(blocks + 2):
        if j < blocks:
            settle(j)
            kernel_grad(j)
            reduce_pass(j)
        if j == 0:
            input_grad()
        if j + 1 < blocks:
            fetch(j + 1)
        if 1 <= j < blocks + 1:
            finish(j - 1)
        if j >= 2:
            share(j - 2)
    input_grad_end()
    gw_ref[...] = total[...]

    @pl.when(has_right)
    def _():
        down().wait_send()
        down_sib().wait_send()

    @pl.when(has_left)
    def _():
        up().wait_send()
        up_sib().wait_send()

    across().wait_send()
    for k in range(n_c):
        relay(k).wait_send()
        if k:
            spread(k).wait_send()
            give(k).wait_send()
    for j in range(blocks):
        drain(j)


def on_device(sizes, inputs, grad_out, weight):
    n_c, n_s = sizes
    _, frames, rows, in_part, cols = inputs.shape
    out_part = grad_out.shape[3]
    in_all = weight.shape[4]
    cfg = (n_c, n_s, frames, rows, in_part, out_part, cols, in_all)
    half = out_part // 2
    first = max(0, 3 - frames)
    taps = 3 - first
    cells = frames * rows * cols
    width = max(LANES, in_part)
    blocks = in_all // width
    grad_rows = taps * 9 * half
    own_count = max(n for n in range(1, n_s + 1) if grad_rows % (16 * n) == 0)
    piece = grad_rows // own_count
    dma = pltpu.SemaphoreType.DMA
    chunk_sem = dma((blocks, own_count))
    vmem = pl.BlockSpec(memory_space=pltpu.VMEM)
    grad_in, total = pl.pallas_call(
        functools.partial(kernel, cfg),
        out_shape=(
            jax.ShapeDtypeStruct((frames, rows, in_part, cols), BF16),
            jax.ShapeDtypeStruct((grad_rows, in_all), BF16),
        ),
        in_specs=[vmem, vmem, pl.BlockSpec(memory_space=pl.ANY)],
        out_specs=(vmem, vmem),
        scratch_shapes=[
            pltpu.VMEM((2, in_all, cells), BF16),
            pltpu.VMEM((frames, out_part, cols), BF16),
            pltpu.VMEM((frames, out_part, cols), BF16),
            pltpu.VMEM((frames, half, cols), BF16),
            pltpu.VMEM((frames, half, cols), BF16),
            pltpu.VMEM((frames, rows, half, cols), BF16),
            pltpu.VMEM((9 * out_part, cells), BF16),
            pltpu.VMEM((2, 9 * half, cells), BF16),
            pltpu.VMEM((taps * 9 * out_part, in_all), BF16),
            pltpu.VMEM((blocks, grad_rows, width), F32),
            pltpu.VMEM((blocks, own_count, piece, width), BF16),
            pltpu.VMEM((blocks, own_count, piece, width), BF16),
            pltpu.VMEM((grad_rows, in_all), BF16),
            pltpu.VMEM((in_all, cells), F32),
            pltpu.VMEM((in_all, cells), BF16),
            pltpu.VMEM((n_c, in_part, cells), BF16),
            dma,
            dma((5,)),
            dma((5,)),
            dma((n_c,)),
            dma((n_c,)),
            dma((n_c,)),
            dma((n_c,)),
            chunk_sem, chunk_sem, chunk_sem, chunk_sem, chunk_sem, chunk_sem, chunk_sem,
            dma((n_c,)),
            dma((n_c,)),
        ],
        compiler_params=pltpu.CompilerParams(
            collective_id=0, has_side_effects=True, vmem_limit_bytes=48 << 20
        ),
    )(
        inputs.reshape(frames, rows, in_part, cols),
        grad_out.reshape(frames, rows, out_part, cols),
        weight.reshape(27 * out_part, in_all),
    )
    scaled = total.astype(F32) * (1.0 / 256.0)
    grad_weight = jnp.pad(
        scaled.reshape(taps, 3, 3, half, in_all), ((first, 0), (0, 0), (0, 0), (0, 0), (0, 0))
    )
    return grad_in.reshape(inputs.shape), grad_weight


def solution(mesh):
    return jax.shard_map(
        functools.partial(on_device, (mesh.shape["chan"], mesh.shape["space"])),
        mesh=mesh,
        in_specs=(
            P("rep", None, "space", "chan", None),
            P("rep", None, "space", "chan", None),
            P(None, None, None, "chan", None),
        ),
        out_specs=(
            P("rep", None, "space", "chan", None),
            P(None, None, None, ("chan", "rep"), None),
        ),
        check_vma=False,
    )
```

```python
import functools

import jax
import jax.numpy as jnp
from jax import lax
from jax.experimental import pallas as pl
from jax.experimental.pallas import tpu as pltpu
from jax.sharding import PartitionSpec as P

MESH = pl.DeviceIdType.MESH
F32 = jnp.float32
BF16 = jnp.bfloat16
LANES = 128
SPLIT = 2


def flip(index, mask, count):
    out, bit = 0, 1
    while bit < count:
        out = out + (((index // bit) + ((mask // bit) % 2)) % 2) * bit
        bit *= 2
    return out


def cut(grad_rows, n_s):
    split = max(n for n in range(1, SPLIT + 1) if grad_rows % (16 * n) == 0)
    share = grad_rows // split
    count = max(n for n in range(1, n_s + 1) if share % (16 * n) == 0)
    return split, count, share // count


def nt(a, b):
    return lax.dot_general(a, b, (((1,), (1,)), ((), ())), preferred_element_type=F32)


def tn(a, b):
    return lax.dot_general(a, b, (((0,), (0,)), ((), ())), preferred_element_type=F32)


def kernel(
    cfg,
    x_ref, g_ref, w_hbm,
    gi_ref, gw_ref,
    act, halo_top, halo_bot, sib_top, sib_bot, sib_rows,
    xd, xw, w_ref, part, right_buf, left_buf, total,
    d_acc, d_send, d_recv,
    w_sem, g_send, g_recv, a_send, a_recv, b_send, b_recv,
    r_send, r_recv, l_send, l_recv, fr_send, fl_send, f_recv, d_ssem, d_rsem,
):
    n_c, n_s, frames, rows, in_part, out_part, cols, in_all = cfg
    half = out_part // 2
    first = max(0, 3 - frames)
    taps = 3 - first
    plane = rows * cols
    cells = frames * plane
    width = max(LANES, in_part)
    blocks = in_all // width
    per = width // in_part
    grad_rows = taps * 9 * half
    split, own_count, piece = cut(grad_rows, n_s)
    units = blocks * split

    chan = lax.axis_index("chan")
    space = lax.axis_index("space")
    rep = lax.axis_index("rep")
    other = 1 - rep
    has_left = space > 0
    has_right = space < n_s - 1
    after = (space + 1) % n_s
    before = (space + n_s - 1) % n_s

    def remote(src, dst, ssem, rsem, **where):
        return pltpu.make_async_remote_copy(
            src_ref=src, dst_ref=dst, send_sem=ssem, recv_sem=rsem,
            device_id=where, device_id_type=MESH,
        )

    weight_copy = pltpu.make_async_copy(
        w_hbm.at[pl.ds(first * 9 * out_part, taps * 9 * out_part)], w_ref, w_sem
    )
    weight_copy.start()

    barrier = pltpu.get_barrier_semaphore()

    def greet(**where):
        pl.semaphore_signal(barrier, inc=1, device_id=where, device_id_type=MESH)

    for k in range(1, n_c):
        greet(chan=flip(chan, k, n_c))
    greet(rep=other)

    @pl.when(has_left)
    def _():
        greet(space=before)
        greet(space=before, rep=other)

    @pl.when(has_right)
    def _():
        greet(space=after)
        greet(space=after, rep=other)

    my_rows = pl.ds(pl.multiple_of(chan * in_part, in_part), in_part)
    for t in range(frames):
        for h in range(rows):
            v = x_ref[t, h].astype(F32)
            at = (t * rows + h) * cols
            act[0, my_rows, at : at + cols] = (v * jax.nn.sigmoid(v)).astype(BF16)

    inner = jnp.logical_and(has_left, has_right)

    @pl.when(inner)
    def _():
        pl.semaphore_wait(barrier, n_c + 4)

    @pl.when(jnp.logical_not(inner))
    def _():
        pl.semaphore_wait(barrier, n_c + (2 if n_s > 1 else 0))

    theirs = pl.ds(pl.multiple_of(other * half, half), half)

    def down():
        return remote(g_ref.at[:, rows - 1], halo_top, g_send.at[0], g_recv.at[0], space=after)

    def down_sib():
        return remote(g_ref.at[:, rows - 1, theirs], sib_top, g_send.at[1], g_recv.at[1], space=after, rep=other)

    def up():
        return remote(g_ref.at[:, 0], halo_bot, g_send.at[2], g_recv.at[2], space=before)

    def up_sib():
        return remote(g_ref.at[:, 0, theirs], sib_bot, g_send.at[3], g_recv.at[3], space=before, rep=other)

    def across():
        return remote(g_ref.at[:, :, theirs], sib_rows, g_send.at[4], g_recv.at[4], rep=other)

    @pl.when(has_right)
    def _():
        down().start()
        down_sib().start()

    @pl.when(has_left)
    def _():
        up().start()
        up_sib().start()

    across().start()

    def chan_rows(k):
        owner = flip(chan, k, n_c)
        return pl.ds(pl.multiple_of(owner * in_part, in_part), in_part)

    def relay(k):
        return remote(act.at[0, chan_rows(k)], act.at[1, chan_rows(k)], b_send.at[k], b_recv.at[k], rep=other)

    def spread(k):
        return remote(act.at[0, my_rows], act.at[0, my_rows], a_send.at[k], a_recv.at[k], chan=flip(chan, k, n_c))

    relay(0).start()
    for k in range(1, n_c):
        spread(k).start()

    @pl.when(has_left)
    def _():
        down().wait_recv()
        down_sib().wait_recv()

    @pl.when(jnp.logical_not(has_left))
    def _():
        halo_top[...] = jnp.zeros_like(halo_top)
        sib_top[...] = jnp.zeros_like(sib_top)

    @pl.when(has_right)
    def _():
        up().wait_recv()
        up_sib().wait_recv()

    @pl.when(jnp.logical_not(has_right))
    def _():
        halo_bot[...] = jnp.zeros_like(halo_bot)
        sib_bot[...] = jnp.zeros_like(sib_bot)

    across().wait_recv()

    def shifts(row):
        v = row.astype(F32)
        lane = lax.broadcasted_iota(jnp.int32, v.shape, 1)
        ahead = jnp.where(lane < cols - 1, pltpu.roll(v, cols - 1, 1), 0.0)
        behind = jnp.where(lane > 0, pltpu.roll(v, 1, 1), 0.0)
        return ahead.astype(BF16), row, behind.astype(BF16)

    def lay(dst, top, bottom, middle):
        for t in range(frames):
            for p in range(rows + 2):
                row = top(t) if p == 0 else bottom(t) if p == rows + 1 else middle(t, p - 1)
                moved = shifts(row)
                for b in range(3):
                    h = p + b - 2
                    if 0 <= h < rows:
                        at = (t * rows + h) * cols
                        for e in range(3):
                            dst(b * 3 + e, at, moved[e])

    def to_sib(i, at, value):
        xw[1, i * half : (i + 1) * half, at : at + cols] = value

    def to_own(i, at, value):
        xd[i * out_part : (i + 1) * out_part, at : at + cols] = value

    lay(to_sib, lambda t: sib_top[t], lambda t: sib_bot[t], lambda t, h: sib_rows[t, h])
    lay(to_own, lambda t: halo_top[t], lambda t: halo_bot[t], lambda t, h: g_ref[t, h])
    for i in range(9):
        xw[0, i * half : (i + 1) * half, :] = xd[
            pl.ds(pl.multiple_of(i * out_part + rep * half, half), half), :
        ]

    def block_of(j):
        return flip(chan // per, j, blocks)

    def kernel_grad(j):
        where = pl.ds(pl.multiple_of(block_of(j) * width, width), width)
        for a in range(first, 3):
            skip, used = (2 - a) * plane, (frames - 2 + a) * plane
            value = nt(xw[0, :, skip:cells], act[0, where, 0:used])
            value = value + nt(xw[1, :, skip:cells], act[1, where, 0:used])
            at = (a - first) * 9 * half
            part[j, at : at + 9 * half, :] = value

    def fetch(j):
        for k in range(j * per, (j + 1) * per):
            if k:
                spread(k).wait_recv()
                relay(k).start()

    def settle(j):
        for k in range(j * per, (j + 1) * per):
            relay(k).wait_recv()

    def rows_of(u, q):
        return pl.ds(pl.multiple_of(((u % split) * own_count + q) * piece, piece), piece)

    def own(u, q):
        return part[u // split, rows_of(u, q), :]

    def go_right(u, q):
        return remote(right_buf.at[u, q], right_buf.at[u, q], r_send.at[u, q], r_recv.at[u, q], space=after)

    def go_left(u, q):
        return remote(left_buf.at[u, q], left_buf.at[u, q], l_send.at[u, q], l_recv.at[u, q], space=before)

    def slot(u, q):
        return total.at[
            rows_of(u, q), pl.ds(pl.multiple_of(block_of(u // split) * width, width), width)
        ]

    def final_right(u, q):
        return remote(slot(u, q), slot(u, q), fr_send.at[u, q], f_recv.at[u, q], space=after)

    def final_left(u, q):
        return remote(slot(u, q), slot(u, q), fl_send.at[u, q], f_recv.at[u, q], space=before)

    def each(count, body):
        def run(i, carry):
            body(i)
            return carry

        lax.fori_loop(0, count, run, 0)

    def live(u):
        return jnp.logical_and(u >= 0, u < units)

    def step_right(u, q):
        @pl.when(has_left)
        def _():
            go_right(u, q).wait_recv()
            right_buf[u, q] = (right_buf[u, q].astype(F32) + own(u, q)).astype(BF16)

        @pl.when(jnp.logical_not(has_left))
        def _():
            right_buf[u, q] = own(u, q).astype(BF16)

        go_right(u, q).start()

    def step_left(u, q):
        @pl.when(has_right)
        def _():
            go_left(u, q).wait_recv()
            left_buf[u, q] = (left_buf[u, q].astype(F32) + own(u, q)).astype(BF16)

        @pl.when(jnp.logical_not(has_right))
        def _():
            left_buf[u, q] = own(u, q).astype(BF16)

        go_left(u, q).start()

    def finish(u, q):
        @pl.when(has_left)
        def _():
            go_right(u, q).wait_recv()
            part[u // split, rows_of(u, q), :] = own(u, q) + right_buf[u, q].astype(F32)

        @pl.when(has_right)
        def _():
            go_left(u, q).wait_recv()
            part[u // split, rows_of(u, q), :] = own(u, q) + left_buf[u, q].astype(F32)

        slot(u, q)[...] = own(u, q).astype(BF16)

        @pl.when(has_right)
        def _():
            final_right(u, q).start()

        @pl.when(has_left)
        def _():
            final_left(u, q).start()

    def settled(q):
        return jnp.maximum(q, n_s - 1 - q)

    def tick(time):
        right_unit = time - space
        left_unit = time - (n_s - 1 - space)

        def reduce(m):
            far = own_count - 1 - m

            @pl.when(jnp.logical_and(space < far, live(right_unit)))
            def _():
                step_right(right_unit, far)

            @pl.when(jnp.logical_and(space > m, live(left_unit)))
            def _():
                step_left(left_unit, m)

        each(own_count, reduce)
        done_unit = time - settled(space)

        @pl.when(jnp.logical_and(space < own_count, live(done_unit)))
        def _():
            finish(done_unit, space)

        def share(q):
            unit = time - settled(q) - jnp.maximum(space - q, q - space)

            @pl.when(jnp.logical_and(q < space, live(unit)))
            def _():
                final_right(unit, q).wait_recv()

                @pl.when(has_right)
                def _():
                    final_right(unit, q).start()

            @pl.when(jnp.logical_and(q > space, live(unit)))
            def _():
                final_left(unit, q).wait_recv()

                @pl.when(has_left)
                def _():
                    final_left(unit, q).start()

        each(own_count, share)

    def drain(u):
        def body(q):
            @pl.when(space < q)
            def _():
                go_right(u, q).wait_send()

            @pl.when(space > q)
            def _():
                go_left(u, q).wait_send()

            @pl.when(jnp.logical_and(space >= q, has_right))
            def _():
                final_right(u, q).wait_send()

            @pl.when(jnp.logical_and(space <= q, has_left))
            def _():
                final_left(u, q).wait_send()

        each(own_count, body)

    def give(k):
        return remote(d_send.at[chan_rows(k)], d_recv.at[k], d_ssem.at[k], d_rsem.at[k], chan=flip(chan, k, n_c))

    def input_grad():
        weight_copy.wait()
        for i in range(0, in_all, width):
            for a in reversed(range(first, 3)):
                at = (a - first) * 9 * out_part
                skip, used = (2 - a) * plane, (frames - 2 + a) * plane
                value = tn(w_ref[at : at + 9 * out_part, i : i + width], xd[:, skip:cells])
                if a < 2:
                    value = value + d_acc[i : i + width, 0:used]
                d_acc[i : i + width, 0:used] = value
            d_send[i : i + width, :] = d_acc[i : i + width, :].astype(BF16)
        for k in range(1, n_c):
            give(k).start()

    def input_grad_end():
        for k in range(1, n_c):
            give(k).wait_recv()
        for t in range(frames):
            for h in range(rows):
                at = (t * rows + h) * cols
                value = d_acc[my_rows, at : at + cols]
                for k in range(1, n_c):
                    value = value + d_recv[k, :, at : at + cols].astype(F32)
                v = x_ref[t, h].astype(F32)
                s = jax.nn.sigmoid(v)
                gi_ref[t, h] = (value * (s * (1.0 + v * (1.0 - s)))).astype(BF16)

    for j in range(blocks):
        settle(j)
        kernel_grad(j)
        each(split, lambda i: tick(j * split + i))
        if j == 0:
            input_grad()
        if j + 1 < blocks:
            fetch(j + 1)
    each(2 * n_s - 2, lambda i: tick(units + i))
    input_grad_end()
    gw_ref[...] = total[...]

    @pl.when(has_right)
    def _():
        down().wait_send()
        down_sib().wait_send()

    @pl.when(has_left)
    def _():
        up().wait_send()
        up_sib().wait_send()

    across().wait_send()
    for k in range(n_c):
        relay(k).wait_send()
        if k:
            spread(k).wait_send()
            give(k).wait_send()
    each(units, drain)


def on_device(sizes, inputs, grad_out, weight):
    n_c, n_s = sizes
    _, frames, rows, in_part, cols = inputs.shape
    out_part = grad_out.shape[3]
    in_all = weight.shape[4]
    cfg = (n_c, n_s, frames, rows, in_part, out_part, cols, in_all)
    half = out_part // 2
    first = max(0, 3 - frames)
    taps = 3 - first
    cells = frames * rows * cols
    width = max(LANES, in_part)
    blocks = in_all // width
    grad_rows = taps * 9 * half
    split, own_count, piece = cut(grad_rows, n_s)
    units = blocks * split
    dma = pltpu.SemaphoreType.DMA
    chunk_sem = dma((units, own_count))
    vmem = pl.BlockSpec(memory_space=pltpu.VMEM)
    grad_in, total = pl.pallas_call(
        functools.partial(kernel, cfg),
        out_shape=(
            jax.ShapeDtypeStruct((frames, rows, in_part, cols), BF16),
            jax.ShapeDtypeStruct((grad_rows, in_all), BF16),
        ),
        in_specs=[vmem, vmem, pl.BlockSpec(memory_space=pl.ANY)],
        out_specs=(vmem, vmem),
        scratch_shapes=[
            pltpu.VMEM((2, in_all, cells), BF16),
            pltpu.VMEM((frames, out_part, cols), BF16),
            pltpu.VMEM((frames, out_part, cols), BF16),
            pltpu.VMEM((frames, half, cols), BF16),
            pltpu.VMEM((frames, half, cols), BF16),
            pltpu.VMEM((frames, rows, half, cols), BF16),
            pltpu.VMEM((9 * out_part, cells), BF16),
            pltpu.VMEM((2, 9 * half, cells), BF16),
            pltpu.VMEM((taps * 9 * out_part, in_all), BF16),
            pltpu.VMEM((blocks, grad_rows, width), F32),
            pltpu.VMEM((units, own_count, piece, width), BF16),
            pltpu.VMEM((units, own_count, piece, width), BF16),
            pltpu.VMEM((grad_rows, in_all), BF16),
            pltpu.VMEM((in_all, cells), F32),
            pltpu.VMEM((in_all, cells), BF16),
            pltpu.VMEM((n_c, in_part, cells), BF16),
            dma,
            dma((5,)),
            dma((5,)),
            dma((n_c,)),
            dma((n_c,)),
            dma((n_c,)),
            dma((n_c,)),
            chunk_sem, chunk_sem, chunk_sem, chunk_sem, chunk_sem, chunk_sem, chunk_sem,
            dma((n_c,)),
            dma((n_c,)),
        ],
        compiler_params=pltpu.CompilerParams(
            collective_id=0, has_side_effects=True, vmem_limit_bytes=48 << 20
        ),
    )(
        inputs.reshape(frames, rows, in_part, cols),
        grad_out.reshape(frames, rows, out_part, cols),
        weight.reshape(27 * out_part, in_all),
    )
    scaled = total.astype(F32) * (1.0 / 256.0)
    grad_weight = jnp.pad(
        scaled.reshape(taps, 3, 3, half, in_all), ((first, 0), (0, 0), (0, 0), (0, 0), (0, 0))
    )
    return grad_in.reshape(inputs.shape), grad_weight


def solution(mesh):
    return jax.shard_map(
        functools.partial(on_device, (mesh.shape["chan"], mesh.shape["space"])),
        mesh=mesh,
        in_specs=(
            P("rep", None, "space", "chan", None),
            P("rep", None, "space", "chan", None),
            P(None, None, None, "chan", None),
        ),
        out_specs=(
            P("rep", None, "space", "chan", None),
            P(None, None, None, ("chan", "rep"), None),
        ),
        check_vma=False,
    )
```

```python
import functools

import jax
import jax.numpy as jnp
from jax import lax
from jax.experimental import pallas as pl
from jax.experimental.pallas import tpu as pltpu
from jax.sharding import PartitionSpec as P

MESH = pl.DeviceIdType.MESH
F32 = jnp.float32
BF16 = jnp.bfloat16
LANES = 128
SPLIT = 3


def flip(index, mask, count):
    out, bit = 0, 1
    while bit < count:
        out = out + (((index // bit) + ((mask // bit) % 2)) % 2) * bit
        bit *= 2
    return out


def cut(grad_rows, n_s):
    split = max(n for n in range(1, SPLIT + 1) if grad_rows % (16 * n) == 0)
    share = grad_rows // split
    count = max(n for n in range(1, n_s + 1) if share % (16 * n) == 0)
    return split, count, share // count


def nt(a, b):
    return lax.dot_general(a, b, (((1,), (1,)), ((), ())), preferred_element_type=F32)


def tn(a, b):
    return lax.dot_general(a, b, (((0,), (0,)), ((), ())), preferred_element_type=F32)


def kernel(
    cfg,
    x_ref, g_ref, w_hbm,
    gi_ref, gw_ref,
    act, halo_top, halo_bot, sib_top, sib_bot, sib_rows,
    xd, xw, w_ref, part, right_buf, left_buf, total,
    d_acc, d_send, d_recv,
    w_sem, g_send, g_recv, a_send, a_recv, b_send, b_recv,
    r_send, r_recv, l_send, l_recv, fr_send, fl_send, f_recv, d_ssem, d_rsem,
):
    n_c, n_s, frames, rows, in_part, out_part, cols, in_all = cfg
    half = out_part // 2
    first = max(0, 3 - frames)
    taps = 3 - first
    plane = rows * cols
    cells = frames * plane
    width = max(LANES, in_part)
    blocks = in_all // width
    per = width // in_part
    grad_rows = taps * 9 * half
    split, own_count, piece = cut(grad_rows, n_s)
    units = blocks * split

    chan = lax.axis_index("chan")
    space = lax.axis_index("space")
    rep = lax.axis_index("rep")
    other = 1 - rep
    has_left = space > 0
    has_right = space < n_s - 1
    after = (space + 1) % n_s
    before = (space + n_s - 1) % n_s

    def remote(src, dst, ssem, rsem, **where):
        return pltpu.make_async_remote_copy(
            src_ref=src, dst_ref=dst, send_sem=ssem, recv_sem=rsem,
            device_id=where, device_id_type=MESH,
        )

    weight_copy = pltpu.make_async_copy(
        w_hbm.at[pl.ds(first * 9 * out_part, taps * 9 * out_part)], w_ref, w_sem
    )
    weight_copy.start()

    barrier = pltpu.get_barrier_semaphore()

    def greet(**where):
        pl.semaphore_signal(barrier, inc=1, device_id=where, device_id_type=MESH)

    for k in range(1, n_c):
        greet(chan=flip(chan, k, n_c))
    greet(rep=other)

    @pl.when(has_left)
    def _():
        greet(space=before)
        greet(space=before, rep=other)

    @pl.when(has_right)
    def _():
        greet(space=after)
        greet(space=after, rep=other)

    my_rows = pl.ds(pl.multiple_of(chan * in_part, in_part), in_part)
    for t in range(frames):
        for h in range(rows):
            v = x_ref[t, h].astype(F32)
            at = (t * rows + h) * cols
            act[0, my_rows, at : at + cols] = (v * jax.nn.sigmoid(v)).astype(BF16)

    inner = jnp.logical_and(has_left, has_right)

    @pl.when(inner)
    def _():
        pl.semaphore_wait(barrier, n_c + 4)

    @pl.when(jnp.logical_not(inner))
    def _():
        pl.semaphore_wait(barrier, n_c + (2 if n_s > 1 else 0))

    theirs = pl.ds(pl.multiple_of(other * half, half), half)

    def down():
        return remote(g_ref.at[:, rows - 1], halo_top, g_send.at[0], g_recv.at[0], space=after)

    def down_sib():
        return remote(g_ref.at[:, rows - 1, theirs], sib_top, g_send.at[1], g_recv.at[1], space=after, rep=other)

    def up():
        return remote(g_ref.at[:, 0], halo_bot, g_send.at[2], g_recv.at[2], space=before)

    def up_sib():
        return remote(g_ref.at[:, 0, theirs], sib_bot, g_send.at[3], g_recv.at[3], space=before, rep=other)

    def across():
        return remote(g_ref.at[:, :, theirs], sib_rows, g_send.at[4], g_recv.at[4], rep=other)

    @pl.when(has_right)
    def _():
        down().start()
        down_sib().start()

    @pl.when(has_left)
    def _():
        up().start()
        up_sib().start()

    across().start()

    def chan_rows(k):
        owner = flip(chan, k, n_c)
        return pl.ds(pl.multiple_of(owner * in_part, in_part), in_part)

    def relay(k):
        return remote(act.at[0, chan_rows(k)], act.at[1, chan_rows(k)], b_send.at[k], b_recv.at[k], rep=other)

    def spread(k):
        return remote(act.at[0, my_rows], act.at[0, my_rows], a_send.at[k], a_recv.at[k], chan=flip(chan, k, n_c))

    relay(0).start()
    for k in range(1, n_c):
        spread(k).start()

    @pl.when(has_left)
    def _():
        down().wait_recv()
        down_sib().wait_recv()

    @pl.when(jnp.logical_not(has_left))
    def _():
        halo_top[...] = jnp.zeros_like(halo_top)
        sib_top[...] = jnp.zeros_like(sib_top)

    @pl.when(has_right)
    def _():
        up().wait_recv()
        up_sib().wait_recv()

    @pl.when(jnp.logical_not(has_right))
    def _():
        halo_bot[...] = jnp.zeros_like(halo_bot)
        sib_bot[...] = jnp.zeros_like(sib_bot)

    across().wait_recv()

    def shifts(row):
        v = row.astype(F32)
        lane = lax.broadcasted_iota(jnp.int32, v.shape, 1)
        ahead = jnp.where(lane < cols - 1, pltpu.roll(v, cols - 1, 1), 0.0)
        behind = jnp.where(lane > 0, pltpu.roll(v, 1, 1), 0.0)
        return ahead.astype(BF16), row, behind.astype(BF16)

    def lay(dst, top, bottom, middle):
        for t in range(frames):
            for p in range(rows + 2):
                row = top(t) if p == 0 else bottom(t) if p == rows + 1 else middle(t, p - 1)
                moved = shifts(row)
                for b in range(3):
                    h = p + b - 2
                    if 0 <= h < rows:
                        at = (t * rows + h) * cols
                        for e in range(3):
                            dst(b * 3 + e, at, moved[e])

    def to_sib(i, at, value):
        xw[1, i * half : (i + 1) * half, at : at + cols] = value

    def to_own(i, at, value):
        xd[i * out_part : (i + 1) * out_part, at : at + cols] = value

    lay(to_sib, lambda t: sib_top[t], lambda t: sib_bot[t], lambda t, h: sib_rows[t, h])
    lay(to_own, lambda t: halo_top[t], lambda t: halo_bot[t], lambda t, h: g_ref[t, h])
    for i in range(9):
        xw[0, i * half : (i + 1) * half, :] = xd[
            pl.ds(pl.multiple_of(i * out_part + rep * half, half), half), :
        ]

    def block_of(j):
        return flip(chan // per, j, blocks)

    def kernel_grad(j):
        where = pl.ds(pl.multiple_of(block_of(j) * width, width), width)
        for a in range(first, 3):
            skip, used = (2 - a) * plane, (frames - 2 + a) * plane
            value = nt(xw[0, :, skip:cells], act[0, where, 0:used])
            value = value + nt(xw[1, :, skip:cells], act[1, where, 0:used])
            at = (a - first) * 9 * half
            part[j, at : at + 9 * half, :] = value

    def fetch(j):
        for k in range(j * per, (j + 1) * per):
            if k:
                spread(k).wait_recv()
                relay(k).start()

    def settle(j):
        for k in range(j * per, (j + 1) * per):
            relay(k).wait_recv()

    def rows_of(u, q):
        return pl.ds(pl.multiple_of(((u % split) * own_count + q) * piece, piece), piece)

    def own(u, q):
        return part[u // split, rows_of(u, q), :]

    def go_right(u, q):
        return remote(right_buf.at[u, q], right_buf.at[u, q], r_send.at[u, q], r_recv.at[u, q], space=after)

    def go_left(u, q):
        return remote(left_buf.at[u, q], left_buf.at[u, q], l_send.at[u, q], l_recv.at[u, q], space=before)

    def slot(u, q):
        return total.at[
            rows_of(u, q), pl.ds(pl.multiple_of(block_of(u // split) * width, width), width)
        ]

    def final_right(u, q):
        return remote(slot(u, q), slot(u, q), fr_send.at[u, q], f_recv.at[u, q], space=after)

    def final_left(u, q):
        return remote(slot(u, q), slot(u, q), fl_send.at[u, q], f_recv.at[u, q], space=before)

    def each(count, body):
        def run(i, carry):
            body(i)
            return carry

        lax.fori_loop(0, count, run, 0)

    def live(u):
        return jnp.logical_and(u >= 0, u < units)

    def step_right(u, q):
        @pl.when(has_left)
        def _():
            go_right(u, q).wait_recv()
            right_buf[u, q] = (right_buf[u, q].astype(F32) + own(u, q)).astype(BF16)

        @pl.when(jnp.logical_not(has_left))
        def _():
            right_buf[u, q] = own(u, q).astype(BF16)

        go_right(u, q).start()

    def step_left(u, q):
        @pl.when(has_right)
        def _():
            go_left(u, q).wait_recv()
            left_buf[u, q] = (left_buf[u, q].astype(F32) + own(u, q)).astype(BF16)

        @pl.when(jnp.logical_not(has_right))
        def _():
            left_buf[u, q] = own(u, q).astype(BF16)

        go_left(u, q).start()

    def finish(u, q):
        @pl.when(has_left)
        def _():
            go_right(u, q).wait_recv()
            part[u // split, rows_of(u, q), :] = own(u, q) + right_buf[u, q].astype(F32)

        @pl.when(has_right)
        def _():
            go_left(u, q).wait_recv()
            part[u // split, rows_of(u, q), :] = own(u, q) + left_buf[u, q].astype(F32)

        slot(u, q)[...] = own(u, q).astype(BF16)

        @pl.when(has_right)
        def _():
            final_right(u, q).start()

        @pl.when(has_left)
        def _():
            final_left(u, q).start()

    def settled(q):
        return jnp.maximum(q, n_s - 1 - q)

    def tick(time):
        right_unit = time - space
        left_unit = time - (n_s - 1 - space)

        def reduce(m):
            far = own_count - 1 - m

            @pl.when(jnp.logical_and(space < far, live(right_unit)))
            def _():
                step_right(right_unit, far)

            @pl.when(jnp.logical_and(space > m, live(left_unit)))
            def _():
                step_left(left_unit, m)

        each(own_count, reduce)
        done_unit = time - settled(space)

        @pl.when(jnp.logical_and(space < own_count, live(done_unit)))
        def _():
            finish(done_unit, space)

        def share(q):
            unit = time - settled(q) - jnp.maximum(space - q, q - space)

            @pl.when(jnp.logical_and(q < space, live(unit)))
            def _():
                final_right(unit, q).wait_recv()

                @pl.when(has_right)
                def _():
                    final_right(unit, q).start()

            @pl.when(jnp.logical_and(q > space, live(unit)))
            def _():
                final_left(unit, q).wait_recv()

                @pl.when(has_left)
                def _():
                    final_left(unit, q).start()

        each(own_count, share)

    def drain(u):
        def body(q):
            @pl.when(space < q)
            def _():
                go_right(u, q).wait_send()

            @pl.when(space > q)
            def _():
                go_left(u, q).wait_send()

            @pl.when(jnp.logical_and(space >= q, has_right))
            def _():
                final_right(u, q).wait_send()

            @pl.when(jnp.logical_and(space <= q, has_left))
            def _():
                final_left(u, q).wait_send()

        each(own_count, body)

    def give(k):
        return remote(d_send.at[chan_rows(k)], d_recv.at[k], d_ssem.at[k], d_rsem.at[k], chan=flip(chan, k, n_c))

    def input_grad():
        weight_copy.wait()
        for i in range(0, in_all, width):
            for a in reversed(range(first, 3)):
                at = (a - first) * 9 * out_part
                skip, used = (2 - a) * plane, (frames - 2 + a) * plane
                value = tn(w_ref[at : at + 9 * out_part, i : i + width], xd[:, skip:cells])
                if a < 2:
                    value = value + d_acc[i : i + width, 0:used]
                d_acc[i : i + width, 0:used] = value
            d_send[i : i + width, :] = d_acc[i : i + width, :].astype(BF16)
        for k in range(1, n_c):
            give(k).start()

    def input_grad_end():
        for k in range(1, n_c):
            give(k).wait_recv()
        for t in range(frames):
            for h in range(rows):
                at = (t * rows + h) * cols
                value = d_acc[my_rows, at : at + cols]
                for k in range(1, n_c):
                    value = value + d_recv[k, :, at : at + cols].astype(F32)
                v = x_ref[t, h].astype(F32)
                s = jax.nn.sigmoid(v)
                gi_ref[t, h] = (value * (s * (1.0 + v * (1.0 - s)))).astype(BF16)

    for j in range(blocks):
        settle(j)
        kernel_grad(j)
        each(split, lambda i: tick(j * split + i))
        if j == 0:
            input_grad()
        if j + 1 < blocks:
            fetch(j + 1)
    each(2 * n_s - 2, lambda i: tick(units + i))
    input_grad_end()
    gw_ref[...] = total[...]

    @pl.when(has_right)
    def _():
        down().wait_send()
        down_sib().wait_send()

    @pl.when(has_left)
    def _():
        up().wait_send()
        up_sib().wait_send()

    across().wait_send()
    for k in range(n_c):
        relay(k).wait_send()
        if k:
            spread(k).wait_send()
            give(k).wait_send()
    each(units, drain)


def on_device(sizes, inputs, grad_out, weight):
    n_c, n_s = sizes
    _, frames, rows, in_part, cols = inputs.shape
    out_part = grad_out.shape[3]
    in_all = weight.shape[4]
    cfg = (n_c, n_s, frames, rows, in_part, out_part, cols, in_all)
    half = out_part // 2
    first = max(0, 3 - frames)
    taps = 3 - first
    cells = frames * rows * cols
    width = max(LANES, in_part)
    blocks = in_all // width
    grad_rows = taps * 9 * half
    split, own_count, piece = cut(grad_rows, n_s)
    units = blocks * split
    dma = pltpu.SemaphoreType.DMA
    chunk_sem = dma((units, own_count))
    vmem = pl.BlockSpec(memory_space=pltpu.VMEM)
    grad_in, total = pl.pallas_call(
        functools.partial(kernel, cfg),
        out_shape=(
            jax.ShapeDtypeStruct((frames, rows, in_part, cols), BF16),
            jax.ShapeDtypeStruct((grad_rows, in_all), BF16),
        ),
        in_specs=[vmem, vmem, pl.BlockSpec(memory_space=pl.ANY)],
        out_specs=(vmem, vmem),
        scratch_shapes=[
            pltpu.VMEM((2, in_all, cells), BF16),
            pltpu.VMEM((frames, out_part, cols), BF16),
            pltpu.VMEM((frames, out_part, cols), BF16),
            pltpu.VMEM((frames, half, cols), BF16),
            pltpu.VMEM((frames, half, cols), BF16),
            pltpu.VMEM((frames, rows, half, cols), BF16),
            pltpu.VMEM((9 * out_part, cells), BF16),
            pltpu.VMEM((2, 9 * half, cells), BF16),
            pltpu.VMEM((taps * 9 * out_part, in_all), BF16),
            pltpu.VMEM((blocks, grad_rows, width), F32),
            pltpu.VMEM((units, own_count, piece, width), BF16),
            pltpu.VMEM((units, own_count, piece, width), BF16),
            pltpu.VMEM((grad_rows, in_all), BF16),
            pltpu.VMEM((in_all, cells), F32),
            pltpu.VMEM((in_all, cells), BF16),
            pltpu.VMEM((n_c, in_part, cells), BF16),
            dma,
            dma((5,)),
            dma((5,)),
            dma((n_c,)),
            dma((n_c,)),
            dma((n_c,)),
            dma((n_c,)),
            chunk_sem, chunk_sem, chunk_sem, chunk_sem, chunk_sem, chunk_sem, chunk_sem,
            dma((n_c,)),
            dma((n_c,)),
        ],
        compiler_params=pltpu.CompilerParams(
            collective_id=0, has_side_effects=True, vmem_limit_bytes=48 << 20
        ),
    )(
        inputs.reshape(frames, rows, in_part, cols),
        grad_out.reshape(frames, rows, out_part, cols),
        weight.reshape(27 * out_part, in_all),
    )
    scaled = total.astype(F32) * (1.0 / 256.0)
    grad_weight = jnp.pad(
        scaled.reshape(taps, 3, 3, half, in_all), ((first, 0), (0, 0), (0, 0), (0, 0), (0, 0))
    )
    return grad_in.reshape(inputs.shape), grad_weight


def solution(mesh):
    return jax.shard_map(
        functools.partial(on_device, (mesh.shape["chan"], mesh.shape["space"])),
        mesh=mesh,
        in_specs=(
            P("rep", None, "space", "chan", None),
            P("rep", None, "space", "chan", None),
            P(None, None, None, "chan", None),
        ),
        out_specs=(
            P("rep", None, "space", "chan", None),
            P(None, None, None, ("chan", "rep"), None),
        ),
        check_vma=False,
    )
```
